32 devices in a mesh: strip: 32 (over z, y, x, core).
Axes of the slice: x: 2, y: 2, z: 4, core: 2. Of those that a mesh axis runs over, the one named last changes fastest.
Arguments:
- features: bfloat16 [64, 1024, 1024], P(None, 'strip'), may hold values from -6 to 6
- row_kernel: bfloat16 [8, 8, 8, 129], replicated, may hold values from -0.1875 to 0.1875
- mix_weight: bfloat16 [64, 64], replicated, may hold values from -0.75 to 0.75
- channel_bias: float32 [64], replicated, may hold values from -3 to 3
Outputs:
- layer_out: bfloat16 [64, 1024, 1024], P(None, 'strip')
The draws below stay inside these ranges and needn't reach their ends.
All inputs are finite; a program needn't handle non-finite values.
Results may differ from the reference program's by a relative error of at most 0.001.
Values may be sent and summed in bfloat16 or wider, within the bound.
A program may use at most 128 MiB of HBM per device.

```python
import jax
import jax.numpy as jnp
from jax import lax

C = 64
GW = 8
HALF = 64
ROWS_DEV = 32
NCOL = 1024
TAPS = 129
GROUPS = 8
ROWS = 1024
N_STRIP = 32


def block_scale(key, extent, split, smallest, largest):
    loudness, own = 1.0, jax.random.fold_in(key, 6)
    for position, shards_of in split:
        heights = jnp.exp(jax.random.uniform(jax.random.fold_in(own, position), (shards_of,), jnp.float32, smallest / len(split), largest / len(split)))
        loudness = loudness * jnp.repeat(heights, extent[position] // shards_of).reshape([-1 if axis == position else 1 for axis in range(len(extent))])
    return loudness


def bell_draw(own_key, dims, deviation, most, cuts=(), dtype=jnp.bfloat16):
    loudness = block_scale(own_key, dims, cuts, -0.22, 0.18) if cuts else 1.0
    drawn = jax.random.normal(own_key, dims, jnp.float32) * deviation * loudness
    return jnp.minimum(jnp.maximum(drawn, -most), most).astype(dtype)


def setup_inputs(seed: int = 0) -> dict:
    arg_keys = jax.random.split(jax.random.key(seed), 5)
    return {
        "features": bell_draw(arg_keys[0], (C, ROWS, NCOL), 1.0, 6.0, ((1, 32),)),
        "row_kernel": bell_draw(arg_keys[1], (GROUPS, GW, GW, TAPS), (GW * TAPS) ** -0.5, 0.1875),
        "mix_weight": bell_draw(arg_keys[2], (C, C), C ** -0.5, 0.75),
        "channel_bias": bell_draw(arg_keys[3], (C,), 0.5, 3.0, (), jnp.float32),
    }


def reference(features, row_kernel, mix_weight, channel_bias):
    grid_rows = ROWS_DEV * N_STRIP
    tap_count = 2 * HALF + 1
    front = row_kernel[..., HALF::-1]
    back = row_kernel[..., 2 * HALF:HALF:-1]
    middle = jnp.zeros((GROUPS, GW, GW, grid_rows - tap_count), jnp.bfloat16)
    filters = jnp.concatenate([front, middle, back], axis=-1).astype(jnp.float32)
    spectra = jnp.fft.rfft(filters, axis=-1)
    grouped = features.astype(jnp.float32).reshape(GROUPS, GW, grid_rows, NCOL)

    def one_group(pair):
        block, spectrum = pair
        block_hat = jnp.fft.rfft(block, axis=1)
        out_hat = jnp.einsum("oif,ifw->ofw", spectrum, block_hat)
        return jnp.fft.irfft(out_hat, n=grid_rows, axis=1)

    conv = lax.map(one_group, (grouped, spectra)).reshape(C, grid_rows, NCOL)
    mixed = jnp.einsum("io,irw->orw", mix_weight.astype(jnp.float32), features.astype(jnp.float32))
    total = conv + mixed + channel_bias[:, None, None]
    return jax.nn.gelu(total).astype(jnp.bfloat16)
```

```python
import jax
import jax.numpy as jnp
from jax import lax
from jax.sharding import PartitionSpec as P

TEAM = 2


def sent(block, axis, team_shift, member_shift):
    count = lax.axis_size(axis)
    route = []
    for i in range(count):
        team, member = divmod(i, TEAM)
        target = ((team + team_shift) * TEAM) % count + (member + member_shift) % TEAM
        route.append((i, target))
    return lax.ppermute(block, axis, route)


def band(row_kernel, out_rows, first, rows):
    tap_count = row_kernel.shape[-1]
    shape = (out_rows, rows, tap_count)
    out_index = lax.broadcasted_iota(jnp.int32, shape, 0)
    in_index = lax.broadcasted_iota(jnp.int32, shape, 1) + first
    tap_index = lax.broadcasted_iota(jnp.int32, shape, 2)
    one_hot = (in_index - out_index == tap_index).astype(row_kernel.dtype)
    banded = jnp.einsum("goct,pit->gopci", row_kernel, one_hot)
    groups, width = row_kernel.shape[:2]
    return banded.reshape(groups, width * out_rows, width * rows)


def local(features, row_kernel, mix_weight, channel_bias):
    channels, strip_rows, columns = features.shape
    groups, width, _, tap_count = row_kernel.shape
    reach = (tap_count - 1) // 2
    team_rows = TEAM * strip_rows
    teams_away = reach // team_rows
    part = columns // TEAM
    member = lax.axis_index("strip") % TEAM
    even = member == 0
    low, high = features[:, :, :part], features[:, :, part:]
    kept = jnp.where(even, low, high)
    other = jnp.where(even, high, low)

    def team_block(team_shift):
        if team_shift == 0:
            same = kept
        else:
            same = sent(kept, "strip", team_shift, 0)
        cross = sent(other, "strip", team_shift, 1)
        first = jnp.where(even, same, cross)
        second = jnp.where(even, cross, same)
        return jnp.concatenate([first, second], axis=1)

    def product(first, rows):
        matrix = band(row_kernel, team_rows, first, rows.shape[1])
        data = rows.reshape(groups, width * rows.shape[1], part)
        return jnp.einsum("gab,gbw->gaw", matrix, data, preferred_element_type=jnp.float32)

    center = team_block(0)
    total = product(reach, center)
    for distance in range(teams_away, 0, -1):
        total += product(reach - distance * team_rows, team_block(distance))
        total += product(reach + distance * team_rows, team_block(-distance))
    mixed = jnp.einsum("io,irw->orw", mix_weight, center, preferred_element_type=jnp.float32)
    total = total.reshape(channels, team_rows, part) + mixed + channel_bias[:, None, None]
    out = jax.nn.gelu(total).astype(jnp.bfloat16)
    top, bottom = out[:, :strip_rows], out[:, strip_rows:]
    mine = jnp.where(even, top, bottom)
    back = sent(jnp.where(even, bottom, top), "strip", 0, 1)
    return jnp.concatenate(
        [jnp.where(even, mine, back), jnp.where(even, back, mine)], axis=2
    )


def solution(mesh):
    return jax.shard_map(
        local,
        mesh=mesh,
        in_specs=(P(None, "strip", None), P(), P(), P()),
        out_specs=P(None, "strip", None),
        check_vma=False,
    )
```
